256 devices in a mesh: col: 8 (over x, core), row: 32 (over y, z).
Axes of the slice: x: 4, y: 4, z: 8, core: 2. Of those that a mesh axis runs over, the one named last changes fastest.
Arguments:
- features: float32 [32768, 512], P(('row', 'col')), may hold values from -6 to 6
- weight: float32 [512, 512], replicated, may hold values from -0.25 to 0.25
- tiles: bfloat16 [8, 32, 48, 128, 128], P('col', 'row'), may hold values from -0.09375 to 0.09375
- tile_rows: int32 [8, 32, 48], P('col', 'row'), may hold values from 0 to 31, as said below
- tile_cols: int32 [8, 32, 48], P('col', 'row'), may hold values from 0 to 7
- tile_count: int32 [8, 32], P('col', 'row'), may hold values from 1 to 48, as said below
- cotangent: bfloat16 [32768, 512], P(('col', 'row')), may hold values from -6 to 6
Outputs:
- aggregated: bfloat16 [32768, 512], P(('col', 'row'))
- grad_x: float32 [32768, 512], P(('row', 'col'))
- grad_w: float32 [512, 512], replicated
The draws below stay inside these ranges and needn't reach their ends.
Inputs may be any that keep to these rules, and one draw needn't show every extreme that they name: `tile_rows`: within one grid block the live slots name distinct tiles. `tile_count`: some grid block has all 48 slots live.
All inputs are finite; a program needn't handle non-finite values.
Results may differ from the reference program's by a relative error of at most 0.0049.
Values may be sent and summed in bfloat16 or wider, within the bound.
No kernel may reach another device: no remote copies, remote signals or barrier semaphores. Data moves between devices by JAX's collectives and lax.ppermute only.
A program may use at most 128 MiB of HBM per device.

```python
import jax
import jax.numpy as jnp
from jax import lax

F = 512
TILE = 128
ROWS_DEV = 128
NODES = 32768
MAXT = 48
N_COL = 8
N_ROW = 32


def tile_layout(key):
    dst_tiles = ROWS_DEV * N_ROW // TILE
    src_tiles = ROWS_DEV * N_COL // TILE
    keys = jax.random.split(jax.random.fold_in(key, 7), N_COL * N_ROW)
    chosen = jax.vmap(lambda one_key: jax.random.permutation(one_key, dst_tiles * src_tiles)[:MAXT])(keys)
    return (chosen.reshape(N_COL, N_ROW, MAXT).astype(jnp.int32), src_tiles)


def draw_tile_rows(key, part):
    chosen, src_tiles = tile_layout(key)
    return (chosen // src_tiles).astype(jnp.int32)


def draw_tile_cols(key, part):
    chosen, src_tiles = tile_layout(key)
    return (chosen % src_tiles).astype(jnp.int32)


def draw_tile_count(key, part):
    first_key = jax.random.fold_in(key, 11)
    second_key = jax.random.fold_in(key, 13)
    raw_draw = jax.random.randint(first_key, (N_COL * N_ROW,), 0, MAXT + 1)
    counts = 1 + raw_draw * raw_draw // (MAXT + 1)
    position = jax.random.randint(second_key, (), 0, N_COL * N_ROW)
    counts = counts.at[position].set(MAXT)
    return counts.reshape(N_COL, N_ROW).astype(jnp.int32)


def steps_of(key, shape, shards, smallest, high):
    level, own = 1.0, jax.random.fold_in(key, 6)
    for axis_at, parts in shards:
        steps = jnp.exp(jax.random.uniform(jax.random.fold_in(own, axis_at), (parts,), jnp.float32, smallest / len(shards), high / len(shards)))
        level = level * jnp.repeat(steps, shape[axis_at] // parts).reshape([-1 if axis == axis_at else 1 for axis in range(len(shape))])
    return level


def centred(rng, shape, deviation, most, pieces=(), kind=jnp.bfloat16):
    loudness = steps_of(rng, shape, pieces, -0.22, 0.18) if pieces else 1.0
    array = jax.random.normal(rng, shape, jnp.float32) * deviation * loudness
    return jnp.minimum(jnp.maximum(array, -most), most).astype(kind)


def setup_inputs(seed: int = 0) -> dict:
    streams_of = jax.random.split(jax.random.key(seed), 8)
    features = centred(streams_of[0], (NODES, F), 1.0, 6.0, ((0, 256),), jnp.float32)
    weight = centred(streams_of[1], (F, F), F ** -0.5, 0.25, (), jnp.float32)
    tiles = centred(streams_of[2], (N_COL, N_ROW, MAXT, TILE, TILE), (ROWS_DEV * N_ROW) ** -0.5, 0.09375, ((0, 8), (1, 32)))
    tile_rows = draw_tile_rows(jax.random.fold_in(streams_of[7], 71), 0)
    tile_cols = draw_tile_cols(jax.random.fold_in(streams_of[7], 71), 0)
    tile_count = draw_tile_count(jax.random.fold_in(streams_of[7], 71), 0)
    cotangent = centred(streams_of[6], (NODES, F), 1.0, 6.0, ((0, 256),))
    return dict(features=features, weight=weight, tiles=tiles, tile_rows=tile_rows, tile_cols=tile_cols, tile_count=tile_count, cotangent=cotangent)


def reference(features, weight, tiles, tile_rows, tile_cols, tile_count, cotangent):
    dst_tiles = ROWS_DEV * N_ROW // TILE
    src_tiles = ROWS_DEV * N_COL // TILE
    projected = jnp.dot(features, weight, precision=lax.Precision.HIGHEST, preferred_element_type=jnp.float32).astype(jnp.bfloat16)
    projected = projected.reshape(N_ROW, src_tiles, TILE, F)
    grads = cotangent.reshape(N_COL, dst_tiles, TILE, F)
    slot_ids = jnp.arange(MAXT, dtype=jnp.int32)

    def step(carry, index):
        agg_sum, back_sum = carry
        col_id = index // N_ROW
        row_id = index % N_ROW
        blocks = tiles[col_id, row_id]
        rows_idx = tile_rows[col_id, row_id]
        cols_idx = tile_cols[col_id, row_id]
        live_slots = slot_ids < tile_count[col_id, row_id]
        picked = projected[row_id][cols_idx]
        tile_terms = jnp.einsum("tab,tbf->taf", blocks.astype(jnp.float32), picked.astype(jnp.float32))
        select_dst = ((rows_idx[None, :] == jnp.arange(dst_tiles, dtype=jnp.int32)[:, None]) & live_slots[None, :]).astype(jnp.float32)
        agg_sum = agg_sum.at[col_id].add(jnp.einsum("it,taf->iaf", select_dst, tile_terms, precision=lax.Precision.HIGHEST))
        picked_g = grads[col_id][rows_idx]
        back_terms = jnp.einsum("tab,taf->tbf", blocks.astype(jnp.float32), picked_g.astype(jnp.float32))
        select_src = ((cols_idx[None, :] == jnp.arange(src_tiles, dtype=jnp.int32)[:, None]) & live_slots[None, :]).astype(jnp.float32)
        back_sum = back_sum.at[row_id].add(jnp.einsum("kt,tbf->kbf", select_src, back_terms, precision=lax.Precision.HIGHEST))
        return (agg_sum, back_sum), None

    start = (jnp.zeros((N_COL, dst_tiles, TILE, F), jnp.float32), jnp.zeros((N_ROW, src_tiles, TILE, F), jnp.float32))
    (agg_sum, back_sum), _ = lax.scan(step, start, jnp.arange(N_COL * N_ROW, dtype=jnp.int32))
    aggregated = agg_sum.reshape(NODES, F).astype(jnp.bfloat16)
    grad_y = back_sum.reshape(NODES, F)
    grad_x = jnp.dot(grad_y, weight.T, precision=lax.Precision.HIGHEST, preferred_element_type=jnp.float32)
    grad_w = jnp.dot(features.T, grad_y, precision=lax.Precision.HIGHEST, preferred_element_type=jnp.float32)
    return (aggregated, grad_x, grad_w)
```

```python
import functools

import jax
import jax.numpy as jnp
from jax import lax
from jax.experimental import pallas as pl
from jax.experimental.pallas import tpu as pltpu
from jax.sharding import Mesh
from jax.sharding import PartitionSpec as P

BF, F32 = jnp.bfloat16, jnp.float32
X, C, Y, Z = 4, 2, 4, 8
MIB = 1 << 20

VM = pl.BlockSpec(memory_space=pltpu.VMEM)
SM = pl.BlockSpec(memory_space=pltpu.SMEM)
ANY = pl.BlockSpec(memory_space=pl.ANY)


def ring(size, step):
    return [(i, (i + step) % size) for i in range(size)]


def hop(value, axis, size, step):
    return lax.ppermute(value, axis, ring(size, step))


def call(kernel, outs, args, specs, scratch=(), flops=0, vmem=48 * MIB):
    size = sum(a.size * a.dtype.itemsize for a in (*args, *outs))
    return pl.pallas_call(
        kernel,
        out_shape=tuple(outs),
        in_specs=list(specs),
        out_specs=tuple(VM for _ in outs),
        scratch_shapes=list(scratch),
        compiler_params=pltpu.CompilerParams(vmem_limit_bytes=vmem),
        cost_estimate=pl.CostEstimate(flops=flops, bytes_accessed=size, transcendentals=0),
    )(*args)


def shape(*dims, dtype=BF):
    return jax.ShapeDtypeStruct(dims, dtype)


def row_place(i, at):
    return ((i >> 3) - at[2]) & 3, ((i & 7) - at[3]) & 7


def col_place(j, at):
    return (((j & 1) - at[1]) & 1) * 4 + (((j >> 1) - at[0]) & 3)


def forward_kernel(rows, cols, count, at, tiles, *refs):
    sources, a_out, b_out = refs[:8], refs[8:12], refs[12:20]
    held, acc, sems = refs[20:]
    copies = [pltpu.make_async_copy(sources[s].at[pl.ds(0, 128)], held.at[s], sems.at[s]) for s in range(8)]
    for c in copies:
        c.start()

    @pl.loop(0, 32)
    def _(i):
        acc[i] = jnp.zeros(acc.shape[1:], F32)

    for c in copies:
        c.wait()

    @pl.loop(0, count[0, 0])
    def _(t):
        k, d = row_place(rows[0, 0, t], at)
        e = k * 8 + d
        s = col_place(cols[0, 0, t], at)
        acc[e] += jnp.dot(tiles[t], held[s], preferred_element_type=F32)

    for k in range(4):

        @pl.loop(0, 8)
        def _(d):
            a_out[k][d] = acc[k * 8 + d, :, :256].astype(BF)

    for d in range(8):

        @pl.loop(0, 4)
        def _(k):
            b_out[d][k] = acc[k * 8 + d, :, 256:].astype(BF)


def backward_kernel(rows, cols, count, at, tiles, *refs):
    a_in, b_in, sources, keep, send = refs[:4], refs[4:12], refs[12:20], refs[20], refs[21]
    ga, gb, held, acc, gw, sems = refs[22:]
    copies = [pltpu.make_async_copy(a_in[k], ga.at[k], sems.at[k]) for k in range(4)]
    copies += [pltpu.make_async_copy(b_in[d], gb.at[d], sems.at[4 + d]) for d in range(8)]
    copies += [
        pltpu.make_async_copy(sources[s].at[pl.ds(128, 128)], held.at[pl.ds(s * 128, 128)], sems.at[12 + s])
        for s in range(8)
    ]
    for c in copies:
        c.start()
    acc[...] = jnp.zeros(acc.shape, F32)
    for c in copies:
        c.wait()
    turn = (((0,), (0,)), ((), ()))

    @pl.loop(0, count[0, 0])
    def _(t):
        k, d = row_place(rows[0, 0, t], at)
        s = pl.multiple_of(col_place(cols[0, 0, t], at) * 128, 128)
        block = jnp.concatenate([ga[k, d], gb[d, k]], axis=-1)
        acc[pl.ds(s, 128)] += lax.dot_general(tiles[t], block, turn, preferred_element_type=F32)

    gw[...] = jnp.zeros(gw.shape, F32)

    @pl.loop(0, 4)
    def _(j):
        part = pl.ds(pl.multiple_of(j * 256, 256), 256)
        left, right = held[part], acc[part]
        high = right.astype(BF)
        low = (right - high.astype(F32)).astype(BF)
        gw[...] += lax.dot_general(left, high, turn, preferred_element_type=F32) + lax.dot_general(
            left, low, turn, preferred_element_type=F32
        )

    x, core, y = at[0], at[1], at[2]
    for n in range(4):
        keep[n, :128] = acc[n * 128 : n * 128 + 128]
        send[n, :128] = acc[512 + n * 128 : 640 + n * 128].astype(BF)
        for m in range(4):
            spot = ((x + n) & 3) * 64 + ((y + m) & 3) * 16
            keep[n, 128 + m * 16 : 144 + m * 16] = gw[pl.ds(pl.multiple_of(core * 256 + spot, 16), 16)]
            send[n, 128 + m * 16 : 144 + m * 16] = gw[
                pl.ds(pl.multiple_of((1 - core) * 256 + spot, 16), 16)
            ].astype(BF)


def core_sum_kernel(keep, came, own, one, two, three):
    for n, out in enumerate((own, one, two, three)):
        out[...] = (keep[n] + came[n].astype(F32)).astype(out.dtype)


def sum_kernel(own, one, two, three, back, gw0, gw1, gw2, gw3):
    total = own[...] + one[...].astype(F32) + two[...].astype(F32) + three[...].astype(F32)
    back[...] = total[:128]
    for m, out in enumerate((gw0, gw1, gw2, gw3)):
        out[...] = total[128 + m * 16 : 144 + m * 16]


def ordered_sum_kernel(at, *refs):
    parts, out, slots = refs[:8], refs[8], refs[9]
    for d in range(8):
        slots[(at[3] + d) & 7] = parts[d][...]
    total = slots[0]
    for d in range(1, 8):
        total = total + slots[d]
    out[...] = total.astype(BF)


def place_kernel(at, mine, other, out):
    x, core, y = at[0], at[1], at[2]
    for n in range(4):
        for m in range(4):
            spot = ((x + n) & 3) * 64 + ((y + m) & 3) * 16
            out[pl.ds(pl.multiple_of(core * 256 + spot, 16), 16)] = mine[n, m].astype(F32)
            out[pl.ds(pl.multiple_of((1 - core) * 256 + spot, 16), 16)] = other[n, m].astype(F32)


def split_sum_kernel(*refs):
    ins, outs = refs[:4], refs[4:]
    for d, out in enumerate(outs):
        total = ins[0][d].astype(F32)
        for r in ins[1:]:
            total = total + r[d].astype(F32)
        out[...] = total.astype(out.dtype)


def join_sum_kernel(own, right, left, *outs):
    for k, out in enumerate(outs):
        total = own[k].astype(F32) + right[k].astype(F32) + left[k].astype(F32)
        out[...] = total.astype(out.dtype)


def add(left, right):
    return (left.astype(F32) + right.astype(F32)).astype(BF)


def ring_gather(value):
    right, left = [value], [value]
    for step in range(4):
        right.append(hop(right[-1], "z", Z, 1))
        if step < 3:
            left.append(hop(left[-1], "z", Z, -1))
    return [value, *left[1:], *right[4:0:-1]]


def fan(values, axis, size):
    got = {k: hop(values[k], axis, size, k) for k in sorted(range(1, size), key=lambda k: -min(k, size - k))}
    return [got[size - k] for k in range(1, size)]


def ring_sum(parts):
    right, left = parts[4], parts[5]
    for step in range(4):
        right = hop(right, "z", Z, 1)
        if step < 3:
            left = hop(left, "z", Z, -1)
            right = add(right, parts[3 - step])
            if step < 2:
                left = add(left, parts[6 + step])
    return right, left


def shards(features, weight, tiles, tile_rows, tile_cols, tile_count, cotangent):
    at = jnp.stack([lax.axis_index(n) for n in ("x", "core", "y", "z")]).astype(jnp.int32)
    slots = tiles[0, 0]
    scalars = (tile_rows, tile_cols, tile_count, at)

    half_a, half_b = cotangent[:, :256], cotangent[:, 256:]
    a_own = jnp.stack(ring_gather(half_a))
    a_all = [a_own, *fan([a_own] * Y, "y", Y)]
    b_own = jnp.stack([half_b, *fan([half_b] * Y, "y", Y)])
    b_all = ring_gather(b_own)

    projected = jnp.dot(features, weight, precision=lax.Precision.HIGHEST, preferred_element_type=F32)
    pair = jnp.concatenate([projected.astype(BF), features.astype(BF)])
    line = [pair, *fan([pair] * X, "x", X)]
    sources = [*line, *[hop(v, "core", C, 1) for v in line]]

    parts = call(
        forward_kernel,
        [shape(8, 128, 256)] * 4 + [shape(4, 128, 256)] * 8,
        (*scalars, slots, *sources),
        [SM] * 4 + [VM] + [ANY] * 8,
        [pltpu.VMEM((8, 128, 512), BF), pltpu.VMEM((32, 128, 512), F32), pltpu.SemaphoreType.DMA((8,))],
        flops=48 * 128 * 128 * 512 * 2,
    )
    a_part, b_part = parts[:4], parts[4:]
    a_sum = call(
        split_sum_kernel,
        [shape(128, 256, dtype=F32)] + [shape(128, 256)] * 7,
        (a_part[0], *fan(a_part, "y", Y)),
        [VM] * 4,
    )
    a_right, a_left = ring_sum(a_sum)
    b_right, b_left = ring_sum(b_part)
    b_sum = call(
        join_sum_kernel,
        [shape(128, 256, dtype=F32)] + [shape(128, 256)] * 3,
        (b_part[0], b_right, b_left),
        [VM] * 3,
    )
    b_came = fan(b_sum, "y", Y)
    a_final = a_sum[0] + a_right.astype(F32) + a_left.astype(F32)
    b_final = b_sum[0] + b_came[0].astype(F32) + b_came[1].astype(F32) + b_came[2].astype(F32)
    aggregated = jnp.concatenate([a_final, b_final], axis=1).astype(BF)

    keep, send = call(
        backward_kernel,
        [shape(4, 192, 512, dtype=F32), shape(4, 192, 512)],
        (*scalars, slots, *a_all, *b_all, *sources),
        [SM] * 4 + [VM] + [ANY] * 20,
        [
            pltpu.VMEM((4, 8, 128, 256), BF),
            pltpu.VMEM((8, 4, 128, 256), BF),
            pltpu.VMEM((1024, 512), BF),
            pltpu.VMEM((1024, 512), F32),
            pltpu.VMEM((512, 512), F32),
            pltpu.SemaphoreType.DMA((20,)),
        ],
        flops=48 * 128 * 128 * 512 * 2 + 1024 * 512 * 512 * 4,
    )
    came = hop(send, "core", C, 1)
    col_parts = call(
        core_sum_kernel, [shape(192, 512, dtype=F32)] + [shape(192, 512)] * 3, (keep, came), [VM] * 2
    )
    grad_y, *gw = call(
        sum_kernel,
        [shape(128, 512, dtype=F32)] + [shape(16, 512, dtype=F32)] * 4,
        (col_parts[0], *fan(col_parts, "x", X)),
        [VM] * 4,
    )
    grad_x = jnp.dot(grad_y, weight.T, precision=lax.Precision.HIGHEST, preferred_element_type=F32)
    gw_came = fan(gw, "y", Y)
    gw_part = gw[0] + gw_came[0] + gw_came[1] + gw_came[2]
    (gw_rows,) = call(
        ordered_sum_kernel,
        [shape(16, 512)],
        (at, gw_part, *fan([gw_part] * Z, "z", Z)),
        [SM] + [VM] * 8,
        [pltpu.VMEM((8, 16, 512), F32)],
    )
    gw_rows = jnp.stack([gw_rows, *fan([gw_rows] * Y, "y", Y)])
    gw_rows = jnp.stack([gw_rows, *fan([gw_rows] * X, "x", X)])
    (grad_w,) = call(
        place_kernel,
        [shape(512, 512, dtype=F32)],
        (at, gw_rows, hop(gw_rows, "core", C, 1)),
        [SM] + [VM] * 2,
    )
    return aggregated, grad_x, grad_w


def solution(mesh):
    grid = Mesh(mesh.devices.reshape(X, C, Y, Z), ("x", "core", "y", "z"))
    col, row = ("x", "core"), ("y", "z")
    placed = (
        P(row + col, None),
        P(),
        P(col, row, None, None, None),
        P(col, row, None),
        P(col, row, None),
        P(col, row),
        P(col + row, None),
    )
    return jax.shard_map(
        shards,
        mesh=grid,
        in_specs=placed,
        out_specs=(P(col + row, None), P(row + col, None), P()),
        check_vma=False,
    )
```

```python
import functools

import jax
import jax.numpy as jnp
from jax import lax
from jax.experimental import pallas as pl
from jax.experimental.pallas import tpu as pltpu
from jax.sharding import Mesh
from jax.sharding import PartitionSpec as P

BF, F32 = jnp.bfloat16, jnp.float32
X, C, Y, Z = 4, 2, 4, 8
MIB = 1 << 20

VM = pl.BlockSpec(memory_space=pltpu.VMEM)
SM = pl.BlockSpec(memory_space=pltpu.SMEM)
ANY = pl.BlockSpec(memory_space=pl.ANY)


def ring(size, step):
    return [(i, (i + step) % size) for i in range(size)]


def hop(value, axis, size, step):
    return lax.ppermute(value, axis, ring(size, step))


def call(kernel, outs, args, specs, scratch=(), flops=0, vmem=48 * MIB):
    size = sum(a.size * a.dtype.itemsize for a in (*args, *outs))
    return pl.pallas_call(
        kernel,
        out_shape=tuple(outs),
        in_specs=list(specs),
        out_specs=tuple(VM for _ in outs),
        scratch_shapes=list(scratch),
        compiler_params=pltpu.CompilerParams(vmem_limit_bytes=vmem),
        cost_estimate=pl.CostEstimate(flops=flops, bytes_accessed=size, transcendentals=0),
    )(*args)


def shape(*dims, dtype=BF):
    return jax.ShapeDtypeStruct(dims, dtype)


def row_place(i, at):
    return ((i >> 3) - at[2]) & 3, ((i & 7) - at[3]) & 7


def col_place(j, at):
    return (((j & 1) - at[1]) & 1) * 4 + (((j >> 1) - at[0]) & 3)


def each_slot(n, place, product, update):
    whole = n >> 2

    @pl.loop(0, whole)
    def _(q):
        group = [place(q * 4 + u) for u in range(4)]
        values = [product(t) for t in group]
        for t, v in zip(group, values):
            update(t, v)

    @pl.loop(whole * 4, n)
    def _(u):
        t = place(u)
        update(t, product(t))


def forward_kernel(rows, cols, count, at, tiles, *refs):
    sources, outs = refs[:8], refs[8:13]
    held, acc, sems = refs[13:]
    copies = [pltpu.make_async_copy(sources[s].at[pl.ds(0, 128)], held.at[s], sems.at[s]) for s in range(8)]
    for c in copies:
        c.start()

    @pl.loop(0, 32)
    def _(i):
        acc[i] = jnp.zeros(acc.shape[1:], F32)

    for c in copies:
        c.wait()

    def product(t):
        return jnp.dot(tiles[t], held[col_place(cols[0, 0, t], at)], preferred_element_type=F32)

    def update(t, value):
        k, d = row_place(rows[0, 0, t], at)
        acc[k * 8 + d] += value

    each_slot(count[0, 0], lambda t: t, product, update)

    own, up, down, far_up, far_down = outs

    @pl.loop(0, 8)
    def _(d):
        own[d] = acc[d].astype(BF)
        up[d] = acc[8 + d].astype(BF)
        down[d] = acc[24 + d].astype(BF)
        far_up[d] = acc[16 + d, :, :256].astype(BF)
        far_down[d] = acc[16 + d, :, 256:].astype(BF)


def relay_kernel(up, came_up, down, came_down, up_out, down_out):
    @pl.loop(0, 8)
    def _(d):
        up_out[d, :, :256] = (up[d, :, :256].astype(F32) + came_up[d].astype(F32)).astype(BF)
        up_out[d, :, 256:] = up[d, :, 256:]
        down_out[d, :, :256] = down[d, :, :256]
        down_out[d, :, 256:] = (down[d, :, 256:].astype(F32) + came_down[d].astype(F32)).astype(BF)


TURN = (((0,), (0,)), ((), ()))


def backward_slots(rows, cols, count, at, tiles, got, acc, chosen, last):
    def choose(t, n):
        far = row_place(rows[0, 0, t], at)[1] == 4
        keep = far if last else jnp.logical_not(far)
        chosen[n] = t
        return n + keep.astype(jnp.int32)

    n = lax.fori_loop(0, count[0, 0], choose, jnp.int32(0))

    def product(t):
        k, d = row_place(rows[0, 0, t], at)
        block = jnp.concatenate([got[0][k], got[1][k]], axis=-1) if last else got[d, k]
        return lax.dot_general(tiles[t], block, TURN, preferred_element_type=F32)

    def update(t, value):
        s = pl.multiple_of(col_place(cols[0, 0, t], at) * 128, 128)
        acc[pl.ds(s, 128)] += value

    each_slot(n, lambda u: chosen[u], product, update)


def backward_near_kernel(rows, cols, count, at, tiles, *refs):
    grads, out = refs[:7], refs[7]
    got, chosen, sems = refs[8:]
    order = (0, 1, 2, 3, 5, 6, 7)
    copies = [pltpu.make_async_copy(grads[n], got.at[d], sems.at[n]) for n, d in enumerate(order)]
    for c in copies:
        c.start()
    out[...] = jnp.zeros(out.shape, F32)
    for c in copies:
        c.wait()
    backward_slots(rows, cols, count, at, tiles, got, out, chosen, False)


def backward_far_kernel(rows, cols, count, at, tiles, first, second, near, *refs):
    sources, keep, send = refs[:8], refs[8], refs[9]
    held, acc, gw, chosen, sems = refs[10:]
    copies = [
        pltpu.make_async_copy(sources[s].at[pl.ds(128, 128)], held.at[pl.ds(s * 128, 128)], sems.at[s])
        for s in range(8)
    ]
    for c in copies:
        c.start()
    acc[...] = near[...]
    backward_slots(rows, cols, count, at, tiles, (first, second), acc, chosen, True)
    for c in copies:
        c.wait()
    gw[...] = jnp.zeros(gw.shape, F32)

    @pl.loop(0, 4)
    def _(j):
        part = pl.ds(pl.multiple_of(j * 256, 256), 256)
        left, right = held[part], acc[part]
        high = right.astype(BF)
        low = (right - high.astype(F32)).astype(BF)
        gw[...] += lax.dot_general(left, high, TURN, preferred_element_type=F32) + lax.dot_general(
            left, low, TURN, preferred_element_type=F32
        )

    x, core = at[0], at[1]
    for n in range(4):
        spot = ((x + n) & 3) * 128
        keep[n, :128] = acc[n * 128 : n * 128 + 128]
        send[n, :128] = acc[512 + n * 128 : 640 + n * 128].astype(BF)
        keep[n, 128:] = gw[pl.ds(pl.multiple_of(spot + core * 64, 64), 64)]
        send[n, 128:] = gw[pl.ds(pl.multiple_of(spot + (1 - core) * 64, 64), 64)].astype(BF)


def core_sum_kernel(keep, came, own, one, two, three):
    for n, out in enumerate((own, one, two, three)):
        out[...] = (keep[n] + came[n].astype(F32)).astype(out.dtype)


def sum_kernel(own, one, two, three, back, gw):
    total = own[...] + one[...].astype(F32) + two[...].astype(F32) + three[...].astype(F32)
    back[...] = total[:128]
    gw[...] = total[128:]


def split_sum_kernel(*refs):
    ins, outs = refs[:3], refs[3:]
    for d, out in enumerate(outs):
        total = ins[0][d].astype(F32)
        for r in ins[1:]:
            total = total + r[d].astype(F32)
        out[...] = total.astype(out.dtype)


def place_kernel(at, *refs):
    pieces, out = refs[:8], refs[8]
    for n in range(4):
        spot = ((at[0] + n) & 3) * 128
        out[pl.ds(pl.multiple_of(spot + at[1] * 64, 64), 64)] = pieces[n][...].astype(F32)
        out[pl.ds(pl.multiple_of(spot + (1 - at[1]) * 64, 64), 64)] = pieces[4 + n][...].astype(F32)


def add(left, right):
    return (left.astype(F32) + right.astype(F32)).astype(BF)


def fan(values, axis, size):
    got = {k: hop(values[k], axis, size, k) for k in sorted(range(1, size), key=lambda k: -min(k, size - k))}
    return [got[size - k] for k in range(1, size)]


def ring_sum(parts):
    right, left = parts[4], parts[5]
    for step in range(4):
        right = hop(right, "z", Z, 1)
        if step < 3:
            left = hop(left, "z", Z, -1)
            right = add(right, parts[3 - step])
            if step < 2:
                left = add(left, parts[6 + step])
    return right, left


def after(value, event):
    return lax.optimization_barrier((value, event))[0]


def swap_sum(value, axis, size, bits, kind):
    sent = value.astype(kind)
    got = [lax.ppermute(sent, axis, [(i, i ^ bit) for i in range(size)]).astype(F32) for bit in bits]
    total = sent.astype(F32) + got[0]
    return total if len(bits) == 1 else total + (got[1] + got[2])


def shards(features, weight, tiles, tile_rows, tile_cols, tile_count, cotangent):
    at = jnp.stack([lax.axis_index(n) for n in ("x", "core", "y", "z")]).astype(jnp.int32)
    scalars = (tile_rows, tile_cols, tile_count)
    slots = tiles[0, 0]

    column = fan([cotangent] * Y, "y", Y)
    projected = jnp.dot(features, weight, precision=lax.Precision.HIGHEST, preferred_element_type=F32)
    pair = jnp.concatenate([projected.astype(BF), features.astype(BF)])
    pair = after(pair, column[0])
    line = [pair, *fan([pair] * X, "x", X)]
    sources = [*line, *[hop(after(v, line[1]), "core", C, 1) for v in line]]

    bundle = jnp.stack([cotangent, *column])
    right, left = [bundle], [bundle]
    right.append(hop(bundle, "z", Z, 1))
    left.append(hop(bundle, "z", Z, -1))
    right.append(hop(right[-1], "z", Z, 1))
    left.append(hop(left[-1], "z", Z, -1))
    parts = call(
        forward_kernel,
        [shape(8, 128, 512)] * 3 + [shape(8, 128, 256)] * 2,
        (*scalars, after(at, (right[1], left[1])), slots, *sources),
        [SM] * 4 + [VM] + [ANY] * 8,
        [pltpu.VMEM((8, 128, 512), BF), pltpu.VMEM((32, 128, 512), F32), pltpu.SemaphoreType.DMA((8,))],
        flops=48 * 128 * 128 * 512 * 2,
    )
    own, up, down, far_up, far_down = parts
    came_up, came_down = hop(far_up, "y", Y, 1), hop(far_down, "y", Y, -1)
    right.append(hop(after(right[-1], own), "z", Z, 1))
    left.append(hop(after(left[-1], own), "z", Z, -1))
    up, down = call(relay_kernel, [shape(8, 128, 512)] * 2, (up, came_up, down, came_down), [VM] * 4)
    came_up, came_down = hop(up, "y", Y, 1), hop(down, "y", Y, -1)
    far = [
        hop(after(right[-1], up)[:, :, :256], "z", Z, 1),
        hop(after(left[-1], up)[:, :, 256:], "z", Z, -1),
    ]

    (near,) = call(
        backward_near_kernel,
        [shape(1024, 512, dtype=F32)],
        (*scalars, at, slots, bundle, *left[1:], *right[3:0:-1]),
        [SM] * 4 + [VM] + [ANY] * 7,
        [pltpu.VMEM((8, 4, 128, 512), BF), pltpu.SMEM((48,), jnp.int32), pltpu.SemaphoreType.DMA((7,))],
        flops=42 * 128 * 128 * 512 * 2,
    )
    keep, send = call(
        backward_far_kernel,
        [shape(4, 192, 512, dtype=F32), shape(4, 192, 512)],
        (*scalars, at, slots, *far, near, *sources),
        [SM] * 4 + [VM] * 4 + [ANY] * 8,
        [
            pltpu.VMEM((1024, 512), BF),
            pltpu.VMEM((1024, 512), F32),
            pltpu.VMEM((512, 512), F32),
            pltpu.SMEM((48,), jnp.int32),
            pltpu.SemaphoreType.DMA((8,)),
        ],
        flops=6 * 128 * 128 * 512 * 2 + 1024 * 512 * 512 * 4,
    )
    came = hop(send, "core", C, 1)
    col_parts = call(
        core_sum_kernel, [shape(192, 512, dtype=F32)] + [shape(192, 512)] * 3, (keep, came), [VM] * 2
    )
    col_came = fan(col_parts, "x", X)

    sums = call(
        split_sum_kernel,
        [shape(128, 512, dtype=BF if d in (4, 5) else F32) for d in range(8)],
        (after(own, col_came[0]), came_up, came_down),
        [VM] * 3,
    )
    from_left, from_right = ring_sum(sums)
    aggregated = (sums[0] + from_left.astype(F32) + from_right.astype(F32)).astype(BF)

    grad_y, gw = call(
        sum_kernel,
        [shape(128, 512, dtype=F32), shape(64, 512, dtype=F32)],
        (col_parts[0], *col_came),
        [VM] * 4,
    )
    gw = swap_sum(gw, "y", Y, (1, 2, 3), F32)
    gw = swap_sum(gw, "z", Z, (1,), F32)
    gw = swap_sum(gw, "z", Z, (2, 4, 6), BF)
    gw = gw.astype(BF)
    gw = [gw, *fan([gw] * X, "x", X)]
    (grad_w,) = call(
        place_kernel,
        [shape(512, 512, dtype=F32)],
        (at, *gw, *[hop(v, "core", C, 1) for v in gw]),
        [SM] + [VM] * 8,
    )
    grad_x = jnp.dot(grad_y, weight.T, precision=lax.Precision.HIGHEST, preferred_element_type=F32)
    return aggregated, grad_x, grad_w


def solution(mesh):
    grid = Mesh(mesh.devices.reshape(X, C, Y, Z), ("x", "core", "y", "z"))
    col, row = ("x", "core"), ("y", "z")
    placed = (
        P(row + col, None),
        P(),
        P(col, row, None, None, None),
        P(col, row, None),
        P(col, row, None),
        P(col, row),
        P(col + row, None),
    )
    return jax.shard_map(
        shards,
        mesh=grid,
        in_specs=placed,
        out_specs=(P(col + row, None), P(row + col, None), P()),
        check_vma=False,
    )
```

```python
import functools

import jax
import jax.numpy as jnp
from jax import lax
from jax.experimental import pallas as pl
from jax.experimental.pallas import tpu as pltpu
from jax.sharding import Mesh
from jax.sharding import PartitionSpec as P

BF, F32 = jnp.bfloat16, jnp.float32
X, C, Y, Z = 4, 2, 4, 8
MIB = 1 << 20

VM = pl.BlockSpec(memory_space=pltpu.VMEM)
SM = pl.BlockSpec(memory_space=pltpu.SMEM)
ANY = pl.BlockSpec(memory_space=pl.ANY)


def ring(size, step):
    return [(i, (i + step) % size) for i in range(size)]


def hop(value, axis, size, step):
    return lax.ppermute(value, axis, ring(size, step))


def call(kernel, outs, args, specs, scratch=(), flops=0, vmem=48 * MIB):
    size = sum(a.size * a.dtype.itemsize for a in (*args, *outs))
    return pl.pallas_call(
        kernel,
        out_shape=tuple(outs),
        in_specs=list(specs),
        out_specs=tuple(VM for _ in outs),
        scratch_shapes=list(scratch),
        compiler_params=pltpu.CompilerParams(vmem_limit_bytes=vmem),
        cost_estimate=pl.CostEstimate(flops=flops, bytes_accessed=size, transcendentals=0),
    )(*args)


def shape(*dims, dtype=BF):
    return jax.ShapeDtypeStruct(dims, dtype)


def row_place(i, at):
    return ((i >> 3) - at[2]) & 3, ((i & 7) - at[3]) & 7


def col_place(j, at):
    return (((j & 1) - at[1]) & 1) * 4 + (((j >> 1) - at[0]) & 3)


def each_slot(n, place, product, update):
    whole = n >> 2

    @pl.loop(0, whole)
    def _(q):
        group = [place(q * 4 + u) for u in range(4)]
        values = [product(t) for t in group]
        for t, v in zip(group, values):
            update(t, v)

    @pl.loop(whole * 4, n)
    def _(u):
        t = place(u)
        update(t, product(t))


def forward_kernel(rows, cols, count, at, tiles, *refs):
    sources, outs = refs[:8], refs[8:13]
    held, acc, sems = refs[13:]
    copies = [pltpu.make_async_copy(sources[s].at[pl.ds(0, 128)], held.at[s], sems.at[s]) for s in range(8)]
    for c in copies:
        c.start()

    @pl.loop(0, 32)
    def _(i):
        acc[i] = jnp.zeros(acc.shape[1:], F32)

    for c in copies:
        c.wait()

    def product(t):
        return jnp.dot(tiles[t], held[col_place(cols[0, 0, t], at)], preferred_element_type=F32)

    def update(t, value):
        k, d = row_place(rows[0, 0, t], at)
        acc[k * 8 + d] += value

    each_slot(count[0, 0], lambda t: t, product, update)

    own, up, down, far_up, far_down = outs

    @pl.loop(0, 8)
    def _(d):
        own[d] = acc[d].astype(BF)
        up[d] = acc[8 + d].astype(BF)
        down[d] = acc[24 + d].astype(BF)
        far_up[d] = acc[16 + d, :, :256].astype(BF)
        far_down[d] = acc[16 + d, :, 256:].astype(BF)


def relay_kernel(up, came_up, down, came_down, up_out, down_out):
    @pl.loop(0, 8)
    def _(d):
        up_out[d, :, :256] = (up[d, :, :256].astype(F32) + came_up[d].astype(F32)).astype(BF)
        up_out[d, :, 256:] = up[d, :, 256:]
        down_out[d, :, :256] = down[d, :, :256]
        down_out[d, :, 256:] = (down[d, :, 256:].astype(F32) + came_down[d].astype(F32)).astype(BF)


TURN = (((0,), (0,)), ((), ()))


def backward_slots(rows, cols, count, at, tiles, got, acc, chosen, last):
    def choose(t, n):
        far = row_place(rows[0, 0, t], at)[1] == 4
        keep = far if last else jnp.logical_not(far)
        chosen[n] = t
        return n + keep.astype(jnp.int32)

    n = lax.fori_loop(0, count[0, 0], choose, jnp.int32(0))

    def product(t):
        k, d = row_place(rows[0, 0, t], at)
        block = jnp.concatenate([got[0][k], got[1][k]], axis=-1) if last else got[d, k]
        return lax.dot_general(tiles[t], block, TURN, preferred_element_type=F32)

    def update(t, value):
        s = pl.multiple_of(col_place(cols[0, 0, t], at) * 128, 128)
        acc[pl.ds(s, 128)] += value

    each_slot(n, lambda u: chosen[u], product, update)


def backward_near_kernel(rows, cols, count, at, tiles, *refs):
    grads, out = refs[:7], refs[7]
    got, chosen, sems = refs[8:]
    order = (0, 1, 2, 3, 5, 6, 7)
    copies = [pltpu.make_async_copy(grads[n], got.at[d], sems.at[n]) for n, d in enumerate(order)]
    for c in copies:
        c.start()
    out[...] = jnp.zeros(out.shape, F32)
    for c in copies:
        c.wait()
    backward_slots(rows, cols, count, at, tiles, got, out, chosen, False)


def backward_far_kernel(rows, cols, count, at, tiles, first, second, near, *refs):
    sources, keep, send = refs[:8], refs[8], refs[9]
    held, acc, split, gw, chosen, sems = refs[10:]
    copies = [
        pltpu.make_async_copy(sources[s].at[pl.ds(128, 128)], held.at[pl.ds(s * 128, 128)], sems.at[s])
        for s in range(8)
    ]
    for c in copies:
        c.start()
    acc[...] = near[...]
    backward_slots(rows, cols, count, at, tiles, (first, second), acc, chosen, True)
    for c in copies:
        c.wait()
    for j in range(8):
        part = pl.ds(j * 128, 128)
        right = acc[part]
        high = right.astype(BF)
        split[0, part] = high
        split[1, part] = (right - high.astype(F32)).astype(BF)

    @pl.loop(0, 2)
    def _(j):
        part = pl.ds(pl.multiple_of(j * 256, 256), 256)
        left = held[:, part]
        gw[part] = lax.dot_general(left, split[0], TURN, preferred_element_type=F32) + lax.dot_general(
            left, split[1], TURN, preferred_element_type=F32
        )

    x, core = at[0], at[1]
    for n in range(4):
        spot = ((x + n) & 3) * 128
        keep[n, :128] = acc[n * 128 : n * 128 + 128]
        send[n, :128] = acc[512 + n * 128 : 640 + n * 128].astype(BF)
        keep[n, 128:] = gw[pl.ds(pl.multiple_of(spot + core * 64, 64), 64)]
        send[n, 128:] = gw[pl.ds(pl.multiple_of(spot + (1 - core) * 64, 64), 64)].astype(BF)


def core_sum_kernel(keep, came, *outs):
    for n in range(4):
        total = keep[n] + came[n].astype(F32)
        outs[n][...] = total[:128].astype(outs[n].dtype)
        outs[4 + n][...] = total[128:].astype(outs[4 + n].dtype)


def split_sum_kernel(*refs):
    ins, outs = refs[:3], refs[3:]
    for d, out in enumerate(outs):
        total = ins[0][d].astype(F32)
        for r in ins[1:]:
            total = total + r[d].astype(F32)
        out[...] = total.astype(out.dtype)


def place_kernel(at, *refs):
    pieces, out = refs[:8], refs[8]
    for n in range(4):
        spot = ((at[0] + n) & 3) * 128
        out[pl.ds(pl.multiple_of(spot + at[1] * 64, 64), 64)] = pieces[n][...].astype(F32)
        out[pl.ds(pl.multiple_of(spot + (1 - at[1]) * 64, 64), 64)] = pieces[4 + n][...].astype(F32)


def total_of(own, came):
    return own + came[0].astype(F32) + came[1].astype(F32) + came[2].astype(F32)


def add(left, right):
    return (left.astype(F32) + right.astype(F32)).astype(BF)


def fan(values, axis, size):
    got = {k: hop(values[k], axis, size, k) for k in sorted(range(1, size), key=lambda k: -min(k, size - k))}
    return [got[size - k] for k in range(1, size)]


def ring_sum(parts):
    right, left = parts[4], parts[5]
    for step in range(4):
        right = hop(right, "z", Z, 1)
        if step < 3:
            left = hop(left, "z", Z, -1)
            right = add(right, parts[3 - step])
            if step < 2:
                left = add(left, parts[6 + step])
    return right, left


def after(value, event):
    return lax.optimization_barrier((value, event))[0]


def swap_sum(value, axis, size, bits, kind):
    sent = value.astype(kind)
    got = [lax.ppermute(sent, axis, [(i, i ^ bit) for i in range(size)]).astype(F32) for bit in bits]
    total = sent.astype(F32) + got[0]
    return total if len(bits) == 1 else total + (got[1] + got[2])


def shards(features, weight, tiles, tile_rows, tile_cols, tile_count, cotangent):
    at = jnp.stack([lax.axis_index(n) for n in ("x", "core", "y", "z")]).astype(jnp.int32)
    scalars = (tile_rows, tile_cols, tile_count)
    slots = tiles[0, 0]

    column = fan([cotangent] * Y, "y", Y)
    projected = jnp.dot(features, weight, precision=lax.Precision.HIGHEST, preferred_element_type=F32)
    pair = jnp.concatenate([projected.astype(BF), features.astype(BF)])
    pair = after(pair, column[0])
    line = [pair, *fan([pair] * X, "x", X)]
    sources = [*line, *[hop(after(v, line[1]), "core", C, 1) for v in line]]

    bundle = jnp.stack([cotangent, *column])
    right, left = [bundle], [bundle]
    right.append(hop(bundle, "z", Z, 1))
    left.append(hop(bundle, "z", Z, -1))
    right.append(hop(right[-1], "z", Z, 1))
    left.append(hop(left[-1], "z", Z, -1))
    parts = call(
        forward_kernel,
        [shape(8, 128, 512)] * 3 + [shape(8, 128, 256)] * 2,
        (*scalars, after(at, (right[1], left[1])), slots, *sources),
        [SM] * 4 + [VM] + [ANY] * 8,
        [pltpu.VMEM((8, 128, 512), BF), pltpu.VMEM((32, 128, 512), F32), pltpu.SemaphoreType.DMA((8,))],
        flops=48 * 128 * 128 * 512 * 2,
    )
    own, up, down, far_up, far_down = parts
    came_up, came_down = hop(far_up, "y", Y, 1), hop(far_down, "y", Y, -1)
    right.append(hop(after(right[-1], own), "z", Z, 1))
    left.append(hop(after(left[-1], own), "z", Z, -1))
    up, down = call(relay_kernel, [shape(8, 128, 512)] * 2, (up, came_up, down, came_down), [VM] * 4)
    came_up, came_down = hop(up, "y", Y, 1), hop(down, "y", Y, -1)
    far = [
        hop(after(right[-1], up)[:, :, :256], "z", Z, 1),
        hop(after(left[-1], up)[:, :, 256:], "z", Z, -1),
    ]

    (near,) = call(
        backward_near_kernel,
        [shape(1024, 512, dtype=F32)],
        (*scalars, at, slots, bundle, *left[1:], *right[3:0:-1]),
        [SM] * 4 + [VM] + [ANY] * 7,
        [pltpu.VMEM((8, 4, 128, 512), BF), pltpu.SMEM((48,), jnp.int32), pltpu.SemaphoreType.DMA((7,))],
        flops=42 * 128 * 128 * 512 * 2,
        vmem=24 * MIB,
    )
    keep, send = call(
        backward_far_kernel,
        [shape(4, 192, 512, dtype=F32), shape(4, 192, 512)],
        (*scalars, at, slots, *far, near, *sources),
        [SM] * 4 + [VM] * 4 + [ANY] * 8,
        [
            pltpu.VMEM((1024, 512), BF),
            pltpu.VMEM((1024, 512), F32),
            pltpu.VMEM((2, 1024, 512), BF),
            pltpu.VMEM((512, 512), F32),
            pltpu.SMEM((48,), jnp.int32),
            pltpu.SemaphoreType.DMA((8,)),
        ],
        flops=6 * 128 * 128 * 512 * 2 + 1024 * 512 * 512 * 4,
        vmem=24 * MIB,
    )
    came = hop(send, "core", C, 1)
    col_parts = call(
        core_sum_kernel,
        [shape(n, 512, dtype=F32 if k == 0 else BF) for n in (128, 64) for k in range(4)],
        (keep, came),
        [VM] * 2,
    )
    back, gw = col_parts[:4], col_parts[4:]
    gw_came = fan(gw, "x", X)

    sums = call(
        split_sum_kernel,
        [shape(128, 512, dtype=BF if d in (4, 5) else F32) for d in range(8)],
        (after(own, gw_came[0]), came_up, came_down),
        [VM] * 3,
    )
    from_left, from_right = ring_sum(sums)
    aggregated = (sums[0] + from_left.astype(F32) + from_right.astype(F32)).astype(BF)

    gw = total_of(gw[0], gw_came)
    gw = swap_sum(gw, "y", Y, (1, 2, 3), F32)
    grad_y = total_of(back[0], fan([after(v, gw) for v in back], "x", X))
    gw = swap_sum(gw, "z", Z, (1,), F32)
    grad_x = jnp.dot(grad_y, weight.T, precision=lax.Precision.HIGHEST, preferred_element_type=F32)
    gw = swap_sum(gw, "z", Z, (2, 4, 6), BF)
    gw = gw.astype(BF)
    gw = [gw, *fan([gw] * X, "x", X)]
    (grad_w,) = call(
        place_kernel,
        [shape(512, 512, dtype=F32)],
        (at, *gw, *[hop(v, "core", C, 1) for v in gw]),
        [SM] + [VM] * 8,
    )
    return aggregated, grad_x, grad_w


def solution(mesh):
    grid = Mesh(mesh.devices.reshape(X, C, Y, Z), ("x", "core", "y", "z"))
    col, row = ("x", "core"), ("y", "z")
    placed = (
        P(row + col, None),
        P(),
        P(col, row, None, None, None),
        P(col, row, None),
        P(col, row, None),
        P(col, row),
        P(col + row, None),
    )
    return jax.shard_map(
        shards,
        mesh=grid,
        in_specs=placed,
        out_specs=(P(col + row, None), P(row + col, None), P()),
        check_vma=False,
    )
```

```python
import functools

import jax
import jax.numpy as jnp
from jax import lax
from jax.experimental import pallas as pl
from jax.experimental.pallas import tpu as pltpu
from jax.sharding import Mesh
from jax.sharding import PartitionSpec as P

BF, F32 = jnp.bfloat16, jnp.float32
X, C, Y, Z = 4, 2, 4, 8
MIB = 1 << 20

VM = pl.BlockSpec(memory_space=pltpu.VMEM)
SM = pl.BlockSpec(memory_space=pltpu.SMEM)
ANY = pl.BlockSpec(memory_space=pl.ANY)


def ring(size, step):
    return [(i, (i + step) % size) for i in range(size)]


def hop(value, axis, size, step):
    return lax.ppermute(value, axis, ring(size, step))


def call(kernel, outs, args, specs, scratch=(), flops=0, vmem=48 * MIB):
    size = sum(a.size * a.dtype.itemsize for a in (*args, *outs))
    return pl.pallas_call(
        kernel,
        out_shape=tuple(outs),
        in_specs=list(specs),
        out_specs=tuple(VM for _ in outs),
        scratch_shapes=list(scratch),
        compiler_params=pltpu.CompilerParams(vmem_limit_bytes=vmem),
        cost_estimate=pl.CostEstimate(flops=flops, bytes_accessed=size, transcendentals=0),
    )(*args)


def shape(*dims, dtype=BF):
    return jax.ShapeDtypeStruct(dims, dtype)


def row_place(i, at):
    return ((i >> 3) - at[2]) & 3, ((i & 7) - at[3]) & 7


def col_place(j, at):
    return (((j & 1) - at[1]) & 1) * 4 + (((j >> 1) - at[0]) & 3)


def each_slot(n, place, product, update):
    whole = n >> 2

    @pl.loop(0, whole)
    def _(q):
        group = [place(q * 4 + u) for u in range(4)]
        values = [product(t) for t in group]
        for t, v in zip(group, values):
            update(t, v)

    @pl.loop(whole * 4, n)
    def _(u):
        t = place(u)
        update(t, product(t))


def forward_kernel(rows, cols, count, at, tiles, *refs):
    sources, outs = refs[:8], refs[8:13]
    held, acc, sems = refs[13:]
    copies = [pltpu.make_async_copy(sources[s].at[pl.ds(0, 128)], held.at[s], sems.at[s]) for s in range(8)]
    for c in copies:
        c.start()

    @pl.loop(0, 32)
    def _(i):
        acc[i] = jnp.zeros(acc.shape[1:], F32)

    for c in copies:
        c.wait()

    def product(t):
        return jnp.dot(tiles[t], held[col_place(cols[0, 0, t], at)], preferred_element_type=F32)

    def update(t, value):
        k, d = row_place(rows[0, 0, t], at)
        acc[k * 8 + d] += value

    each_slot(count[0, 0], lambda t: t, product, update)

    own, up, down, far_up, far_down = outs

    @pl.loop(0, 8)
    def _(d):
        own[d] = acc[d].astype(BF)
        up[d] = acc[8 + d].astype(BF)
        down[d] = acc[24 + d].astype(BF)
        far_up[d] = acc[16 + d, :, :256].astype(BF)
        far_down[d] = acc[16 + d, :, 256:].astype(BF)


def relay_kernel(up, came_up, down, came_down, up_out, down_out):
    @pl.loop(0, 8)
    def _(d):
        up_out[d, :, :256] = (up[d, :, :256].astype(F32) + came_up[d].astype(F32)).astype(BF)
        up_out[d, :, 256:] = up[d, :, 256:]
        down_out[d, :, :256] = down[d, :, :256]
        down_out[d, :, 256:] = (down[d, :, 256:].astype(F32) + came_down[d].astype(F32)).astype(BF)


TURN = (((0,), (0,)), ((), ()))


def backward_slots(rows, cols, count, at, tiles, got, acc, chosen, last):
    def choose(t, n):
        far = row_place(rows[0, 0, t], at)[1] == 4
        keep = far if last else jnp.logical_not(far)
        chosen[n] = t
        return n + keep.astype(jnp.int32)

    n = lax.fori_loop(0, count[0, 0], choose, jnp.int32(0))

    def product(t):
        k, d = row_place(rows[0, 0, t], at)
        block = jnp.concatenate([got[0][k], got[1][k]], axis=-1) if last else got[d, k]
        return lax.dot_general(tiles[t], block, TURN, preferred_element_type=F32)

    def update(t, value):
        s = pl.multiple_of(col_place(cols[0, 0, t], at) * 128, 128)
        acc[pl.ds(s, 128)] += value

    each_slot(n, lambda u: chosen[u], product, update)


def backward_near_kernel(rows, cols, count, at, tiles, *refs):
    grads, out = refs[:7], refs[7]
    got, chosen, sems = refs[8:]
    order = (0, 1, 2, 3, 5, 6, 7)
    copies = [pltpu.make_async_copy(grads[n], got.at[d], sems.at[n]) for n, d in enumerate(order)]
    for c in copies:
        c.start()
    out[...] = jnp.zeros(out.shape, F32)
    for c in copies:
        c.wait()
    backward_slots(rows, cols, count, at, tiles, got, out, chosen, False)


def backward_far_kernel(rows, cols, count, at, tiles, first, second, near, *refs):
    sources, keep, send = refs[:8], refs[8], refs[9]
    held, acc, split, gw, chosen, sems = refs[10:]
    copies = [
        pltpu.make_async_copy(sources[s].at[pl.ds(128, 128)], held.at[pl.ds(s * 128, 128)], sems.at[s])
        for s in range(8)
    ]
    for c in copies:
        c.start()
    acc[...] = near[...]
    backward_slots(rows, cols, count, at, tiles, (first, second), acc, chosen, True)
    for c in copies:
        c.wait()
    for j in range(8):
        part = pl.ds(j * 128, 128)
        right = acc[part]
        high = right.astype(BF)
        split[0, part] = high
        split[1, part] = (right - high.astype(F32)).astype(BF)

    @pl.loop(0, 2)
    def _(j):
        part = pl.ds(pl.multiple_of(j * 256, 256), 256)
        left = held[:, part]
        gw[part] = lax.dot_general(left, split[0], TURN, preferred_element_type=F32) + lax.dot_general(
            left, split[1], TURN, preferred_element_type=F32
        )

    x, core = at[0], at[1]
    for n in range(4):
        spot = ((x + n) & 3) * 128
        keep[n, :128] = acc[n * 128 : n * 128 + 128]
        send[n, :128] = acc[512 + n * 128 : 640 + n * 128].astype(BF)
        keep[n, 128:] = gw[pl.ds(pl.multiple_of(spot + core * 64, 64), 64)]
        send[n, 128:] = gw[pl.ds(pl.multiple_of(spot + (1 - core) * 64, 64), 64)].astype(BF)


def core_sum_kernel(keep, came, *outs):
    for n in range(4):
        total = keep[n] + came[n].astype(F32)
        outs[n][...] = total[:128].astype(outs[n].dtype)
        outs[4 + n][...] = total[128:].astype(outs[4 + n].dtype)


def split_sum_kernel(*refs):
    ins, outs = refs[:3], refs[3:]
    for d, out in enumerate(outs):
        total = ins[0][d].astype(F32)
        for r in ins[1:]:
            total = total + r[d].astype(F32)
        out[...] = total.astype(out.dtype)


def place_kernel(at, *refs):
    pieces, out = refs[:8], refs[8]
    for n in range(4):
        spot = ((at[0] + n) & 3) * 128
        out[pl.ds(pl.multiple_of(spot + at[1] * 64, 64), 64)] = pieces[n][...].astype(F32)
        out[pl.ds(pl.multiple_of(spot + (1 - at[1]) * 64, 64), 64)] = pieces[4 + n][...].astype(F32)


def total_of(own, came):
    return own + came[0].astype(F32) + came[1].astype(F32) + came[2].astype(F32)


def add(left, right):
    return (left.astype(F32) + right.astype(F32)).astype(BF)


def fan(values, axis, size):
    got = {k: hop(values[k], axis, size, k) for k in sorted(range(1, size), key=lambda k: -min(k, size - k))}
    return [got[size - k] for k in range(1, size)]


def ring_sum(parts):
    right, left = parts[4], parts[5]
    for step in range(4):
        right = hop(right, "z", Z, 1)
        if step < 3:
            left = hop(left, "z", Z, -1)
            right = add(right, parts[3 - step])
            if step < 2:
                left = add(left, parts[6 + step])
    return right, left


def after(value, event):
    return lax.optimization_barrier((value, event))[0]


def swap_sum(value, axis, size, bits, kind):
    sent = value.astype(kind)
    got = [lax.ppermute(sent, axis, [(i, i ^ bit) for i in range(size)]).astype(F32) for bit in bits]
    total = sent.astype(F32) + got[0]
    return total if len(bits) == 1 else total + (got[1] + got[2])


def shards(features, weight, tiles, tile_rows, tile_cols, tile_count, cotangent):
    at = jnp.stack([lax.axis_index(n) for n in ("x", "core", "y", "z")]).astype(jnp.int32)
    scalars = (tile_rows, tile_cols, tile_count)
    slots = tiles[0, 0]

    column = fan([cotangent] * Y, "y", Y)
    projected = jnp.dot(features, weight, precision=lax.Precision.HIGH, preferred_element_type=F32)
    pair = jnp.concatenate([projected.astype(BF), features.astype(BF)])
    pair = after(pair, column[0])
    line = [pair, *fan([pair] * X, "x", X)]
    sources = [*line, *[hop(after(v, line[1]), "core", C, 1) for v in line]]

    bundle = jnp.stack([cotangent, *column])
    right, left = [bundle], [bundle]
    right.append(hop(bundle, "z", Z, 1))
    left.append(hop(bundle, "z", Z, -1))
    right.append(hop(right[-1], "z", Z, 1))
    left.append(hop(left[-1], "z", Z, -1))
    parts = call(
        forward_kernel,
        [shape(8, 128, 512)] * 3 + [shape(8, 128, 256)] * 2,
        (*scalars, after(at, (right[1], left[1])), slots, *sources),
        [SM] * 4 + [VM] + [ANY] * 8,
        [pltpu.VMEM((8, 128, 512), BF), pltpu.VMEM((32, 128, 512), F32), pltpu.SemaphoreType.DMA((8,))],
        flops=48 * 128 * 128 * 512 * 2,
    )
    own, up, down, far_up, far_down = parts
    came_up, came_down = hop(far_up, "y", Y, 1), hop(far_down, "y", Y, -1)
    right.append(hop(after(right[-1], own), "z", Z, 1))
    left.append(hop(after(left[-1], own), "z", Z, -1))
    up, down = call(relay_kernel, [shape(8, 128, 512)] * 2, (up, came_up, down, came_down), [VM] * 4)
    came_up, came_down = hop(up, "y", Y, 1), hop(down, "y", Y, -1)
    far = [
        hop(after(right[-1], up)[:, :, :256], "z", Z, 1),
        hop(after(left[-1], up)[:, :, 256:], "z", Z, -1),
    ]

    (near,) = call(
        backward_near_kernel,
        [shape(1024, 512, dtype=F32)],
        (*scalars, at, slots, bundle, *left[1:], *right[3:0:-1]),
        [SM] * 4 + [VM] + [ANY] * 7,
        [pltpu.VMEM((8, 4, 128, 512), BF), pltpu.SMEM((48,), jnp.int32), pltpu.SemaphoreType.DMA((7,))],
        flops=42 * 128 * 128 * 512 * 2,
        vmem=24 * MIB,
    )
    keep, send = call(
        backward_far_kernel,
        [shape(4, 192, 512, dtype=F32), shape(4, 192, 512)],
        (*scalars, at, slots, *far, near, *sources),
        [SM] * 4 + [VM] * 4 + [ANY] * 8,
        [
            pltpu.VMEM((1024, 512), BF),
            pltpu.VMEM((1024, 512), F32),
            pltpu.VMEM((2, 1024, 512), BF),
            pltpu.VMEM((512, 512), F32),
            pltpu.SMEM((48,), jnp.int32),
            pltpu.SemaphoreType.DMA((8,)),
        ],
        flops=6 * 128 * 128 * 512 * 2 + 1024 * 512 * 512 * 4,
        vmem=24 * MIB,
    )
    came = hop(send, "core", C, 1)
    col_parts = call(
        core_sum_kernel,
        [shape(n, 512, dtype=F32 if k == 0 else BF) for n in (128, 64) for k in range(4)],
        (keep, came),
        [VM] * 2,
    )
    back, gw = col_parts[:4], col_parts[4:]
    gw_came = fan(gw, "x", X)

    sums = call(
        split_sum_kernel,
        [shape(128, 512, dtype=BF if d in (4, 5) else F32) for d in range(8)],
        (after(own, gw_came[0]), came_up, came_down),
        [VM] * 3,
    )
    from_left, from_right = ring_sum(sums)
    aggregated = (sums[0] + from_left.astype(F32) + from_right.astype(F32)).astype(BF)

    gw = total_of(gw[0], gw_came)
    gw = swap_sum(gw, "y", Y, (1, 2, 3), F32)
    grad_y = total_of(back[0], fan([after(v, gw) for v in back], "x", X))
    gw = swap_sum(gw, "z", Z, (1,), F32)
    grad_x = jnp.dot(grad_y, weight.T, precision=lax.Precision.HIGH, preferred_element_type=F32)
    gw = swap_sum(gw, "z", Z, (2, 4, 6), BF)
    gw = gw.astype(BF)
    gw = [gw, *fan([gw] * X, "x", X)]
    (grad_w,) = call(
        place_kernel,
        [shape(512, 512, dtype=F32)],
        (at, *gw, *[hop(v, "core", C, 1) for v in gw]),
        [SM] + [VM] * 8,
    )
    return aggregated, grad_x, grad_w


def solution(mesh):
    grid = Mesh(mesh.devices.reshape(X, C, Y, Z), ("x", "core", "y", "z"))
    col, row = ("x", "core"), ("y", "z")
    placed = (
        P(row + col, None),
        P(),
        P(col, row, None, None, None),
        P(col, row, None),
        P(col, row, None),
        P(col, row),
        P(col + row, None),
    )
    return jax.shard_map(
        shards,
        mesh=grid,
        in_specs=placed,
        out_specs=(P(col + row, None), P(row + col, None), P()),
        check_vma=False,
    )
```

```python
import functools

import jax
import jax.numpy as jnp
from jax import lax
from jax.experimental import pallas as pl
from jax.experimental.pallas import tpu as pltpu
from jax.sharding import Mesh
from jax.sharding import PartitionSpec as P

BF, F32 = jnp.bfloat16, jnp.float32
X, C, Y, Z = 4, 2, 4, 8
MIB = 1 << 20

VM = pl.BlockSpec(memory_space=pltpu.VMEM)
SM = pl.BlockSpec(memory_space=pltpu.SMEM)
ANY = pl.BlockSpec(memory_space=pl.ANY)


def ring(size, step):
    return [(i, (i + step) % size) for i in range(size)]


def hop(value, axis, size, step):
    return lax.ppermute(value, axis, ring(size, step))


def call(kernel, outs, args, specs, scratch=(), flops=0, vmem=48 * MIB):
    size = sum(a.size * a.dtype.itemsize for a in (*args, *outs))
    return pl.pallas_call(
        kernel,
        out_shape=tuple(outs),
        in_specs=list(specs),
        out_specs=tuple(VM for _ in outs),
        scratch_shapes=list(scratch),
        compiler_params=pltpu.CompilerParams(vmem_limit_bytes=vmem),
        cost_estimate=pl.CostEstimate(flops=flops, bytes_accessed=size, transcendentals=0),
    )(*args)


def shape(*dims, dtype=BF):
    return jax.ShapeDtypeStruct(dims, dtype)


def row_place(i, at):
    return ((i >> 3) - at[2]) & 3, ((i & 7) - at[3]) & 7


def col_place(j, at):
    return (((j & 1) - at[1]) & 1) * 4 + (((j >> 1) - at[0]) & 3)


def each_slot(n, place, product, update):
    whole = n >> 1

    @pl.loop(0, whole)
    def _(q):
        group = [place(q * 2 + u) for u in range(2)]
        values = [product(t) for t in group]
        for t, v in zip(group, values):
            update(t, v)

    @pl.loop(whole * 2, n)
    def _(u):
        t = place(u)
        update(t, product(t))


def forward_kernel(rows, cols, count, at, tiles, *refs):
    sources, outs = refs[:8], refs[8:13]
    held, acc, sems = refs[13:]
    copies = [pltpu.make_async_copy(sources[s].at[pl.ds(0, 128)], held.at[s], sems.at[s]) for s in range(8)]
    for c in copies:
        c.start()

    @pl.loop(0, 32)
    def _(i):
        acc[i] = jnp.zeros(acc.shape[1:], F32)

    for c in copies:
        c.wait()

    def product(t):
        return jnp.dot(tiles[t], held[col_place(cols[0, 0, t], at)], preferred_element_type=F32)

    def update(t, value):
        k, d = row_place(rows[0, 0, t], at)
        acc[k * 8 + d] += value

    each_slot(count[0, 0], lambda t: t, product, update)

    own, up, down, far_up, far_down = outs

    @pl.loop(0, 8)
    def _(d):
        own[d] = acc[d].astype(BF)
        up[d] = acc[8 + d].astype(BF)
        down[d] = acc[24 + d].astype(BF)
        far_up[d] = acc[16 + d, :, :256].astype(BF)
        far_down[d] = acc[16 + d, :, 256:].astype(BF)


def relay_kernel(up, came_up, down, came_down, up_out, down_out):
    @pl.loop(0, 8)
    def _(d):
        up_out[d, :, :256] = (up[d, :, :256].astype(F32) + came_up[d].astype(F32)).astype(BF)
        up_out[d, :, 256:] = up[d, :, 256:]
        down_out[d, :, :256] = down[d, :, :256]
        down_out[d, :, 256:] = (down[d, :, 256:].astype(F32) + came_down[d].astype(F32)).astype(BF)


TURN = (((0,), (0,)), ((), ()))


def backward_slots(rows, cols, count, at, tiles, got, acc, chosen, last):
    def choose(t, n):
        far = row_place(rows[0, 0, t], at)[1] == 4
        keep = far if last else jnp.logical_not(far)
        chosen[n] = t
        return n + keep.astype(jnp.int32)

    n = lax.fori_loop(0, count[0, 0], choose, jnp.int32(0))

    def product(t):
        k, d = row_place(rows[0, 0, t], at)
        block = jnp.concatenate([got[0][k], got[1][k]], axis=-1) if last else got[d, k]
        return lax.dot_general(tiles[t], block, TURN, preferred_element_type=F32)

    def update(t, value):
        s = pl.multiple_of(col_place(cols[0, 0, t], at) * 128, 128)
        acc[pl.ds(s, 128)] += value

    each_slot(n, lambda u: chosen[u], product, update)


def backward_near_kernel(rows, cols, count, at, tiles, *refs):
    grads, out = refs[:7], refs[7]
    got, chosen, sems = refs[8:]
    order = (0, 1, 2, 3, 5, 6, 7)
    copies = [pltpu.make_async_copy(grads[n], got.at[d], sems.at[n]) for n, d in enumerate(order)]
    for c in copies:
        c.start()

    @pl.loop(0, 16)
    def _(j):
        out[pl.ds(pl.multiple_of(j * 64, 64), 64)] = jnp.zeros((64, 512), F32)

    for c in copies:
        c.wait()
    backward_slots(rows, cols, count, at, tiles, got, out, chosen, False)


def backward_far_kernel(rows, cols, count, at, tiles, first, second, near, *refs):
    sources, keep, send = refs[:8], refs[8], refs[9]
    held, acc, split, gw, chosen, sems = refs[10:]
    copies = [
        pltpu.make_async_copy(sources[s].at[pl.ds(128, 128)], held.at[pl.ds(s * 128, 128)], sems.at[s])
        for s in range(8)
    ]
    for c in copies:
        c.start()

    @pl.loop(0, 16)
    def _(j):
        part = pl.ds(pl.multiple_of(j * 64, 64), 64)
        acc[part] = near[part]

    backward_slots(rows, cols, count, at, tiles, (first, second), acc, chosen, True)
    for c in copies:
        c.wait()
    @pl.loop(0, 16)
    def _(j):
        part = pl.ds(pl.multiple_of(j * 64, 64), 64)
        right = acc[part]
        high = right.astype(BF)
        split[0, part] = high
        split[1, part] = (right - high.astype(F32)).astype(BF)

    @pl.loop(0, 4)
    def _(j):
        part = pl.ds(pl.multiple_of(j * 128, 128), 128)
        left = held[:, part]
        gw[part] = lax.dot_general(left, split[0], TURN, preferred_element_type=F32) + lax.dot_general(
            left, split[1], TURN, preferred_element_type=F32
        )

    x, core = at[0], at[1]

    @pl.loop(0, 4)
    def _(n):
        spot = ((x + n) & 3) * 128
        keep[n, :128] = acc[pl.ds(pl.multiple_of(n * 128, 128), 128)]
        send[n, :128] = acc[pl.ds(pl.multiple_of(512 + n * 128, 128), 128)].astype(BF)
        keep[n, 128:] = gw[pl.ds(pl.multiple_of(spot + core * 64, 64), 64)]
        send[n, 128:] = gw[pl.ds(pl.multiple_of(spot + (1 - core) * 64, 64), 64)].astype(BF)


def core_sum_kernel(keep, came, *outs):
    for n in range(4):
        total = keep[n] + came[n].astype(F32)
        outs[n][...] = total[:128].astype(outs[n].dtype)
        outs[4 + n][...] = total[128:].astype(outs[4 + n].dtype)


def split_sum_kernel(*refs):
    ins, outs = refs[:3], refs[3:]

    @pl.loop(0, 4)
    def _(j):
        part = pl.ds(pl.multiple_of(j * 32, 32), 32)
        for d, out in enumerate(outs):
            total = ins[0][d, part].astype(F32)
            for r in ins[1:]:
                total = total + r[d, part].astype(F32)
            out[part] = total.astype(out.dtype)


def place_kernel(at, *refs):
    pieces, out = refs[:8], refs[8]
    for n in range(4):
        spot = ((at[0] + n) & 3) * 128
        out[pl.ds(pl.multiple_of(spot + at[1] * 64, 64), 64)] = pieces[n][...].astype(F32)
        out[pl.ds(pl.multiple_of(spot + (1 - at[1]) * 64, 64), 64)] = pieces[4 + n][...].astype(F32)


def total_of(own, came):
    return own + came[0].astype(F32) + came[1].astype(F32) + came[2].astype(F32)


def add(left, right):
    return (left.astype(F32) + right.astype(F32)).astype(BF)


def fan(values, axis, size):
    got = {k: hop(values[k], axis, size, k) for k in sorted(range(1, size), key=lambda k: -min(k, size - k))}
    return [got[size - k] for k in range(1, size)]


def ring_sum(parts):
    right, left = parts[4], parts[5]
    for step in range(4):
        right = hop(right, "z", Z, 1)
        if step < 3:
            left = hop(left, "z", Z, -1)
            right = add(right, parts[3 - step])
            if step < 2:
                left = add(left, parts[6 + step])
    return right, left


def after(value, event):
    return lax.optimization_barrier((value, event))[0]


def swap_sum(value, axis, size, bits, kind):
    sent = value.astype(kind)
    got = [lax.ppermute(sent, axis, [(i, i ^ bit) for i in range(size)]).astype(F32) for bit in bits]
    total = sent.astype(F32) + got[0]
    return total if len(bits) == 1 else total + (got[1] + got[2])


def shards(features, weight, tiles, tile_rows, tile_cols, tile_count, cotangent):
    at = jnp.stack([lax.axis_index(n) for n in ("x", "core", "y", "z")]).astype(jnp.int32)
    scalars = (tile_rows, tile_cols, tile_count)
    slots = tiles[0, 0]

    column = fan([cotangent] * Y, "y", Y)
    projected = jnp.dot(features, weight, precision=lax.Precision.HIGH, preferred_element_type=F32)
    pair = jnp.concatenate([projected.astype(BF), features.astype(BF)])
    pair = after(pair, column[0])
    line = [pair, *fan([pair] * X, "x", X)]
    sources = [*line, *[hop(after(v, line[1]), "core", C, 1) for v in line]]

    bundle = jnp.stack([cotangent, *column])
    right, left = [bundle], [bundle]
    right.append(hop(bundle, "z", Z, 1))
    left.append(hop(bundle, "z", Z, -1))
    right.append(hop(right[-1], "z", Z, 1))
    left.append(hop(left[-1], "z", Z, -1))
    parts = call(
        forward_kernel,
        [shape(8, 128, 512)] * 3 + [shape(8, 128, 256)] * 2,
        (*scalars, after(at, (right[1], left[1])), slots, *sources),
        [SM] * 4 + [VM] + [ANY] * 8,
        [pltpu.VMEM((8, 128, 512), BF), pltpu.VMEM((32, 128, 512), F32), pltpu.SemaphoreType.DMA((8,))],
        flops=48 * 128 * 128 * 512 * 2,
    )
    own, up, down, far_up, far_down = parts
    came_up, came_down = hop(far_up, "y", Y, 1), hop(far_down, "y", Y, -1)
    right.append(hop(after(right[-1], own), "z", Z, 1))
    left.append(hop(after(left[-1], own), "z", Z, -1))
    up, down = call(relay_kernel, [shape(8, 128, 512)] * 2, (up, came_up, down, came_down), [VM] * 4)
    came_up, came_down = hop(up, "y", Y, 1), hop(down, "y", Y, -1)
    far = [
        hop(after(right[-1], up)[:, :, :256], "z", Z, 1),
        hop(after(left[-1], up)[:, :, 256:], "z", Z, -1),
    ]

    (near,) = call(
        backward_near_kernel,
        [shape(1024, 512, dtype=F32)],
        (*scalars, at, slots, bundle, *left[1:], *right[3:0:-1]),
        [SM] * 4 + [VM] + [ANY] * 7,
        [pltpu.VMEM((8, 4, 128, 512), BF), pltpu.SMEM((48,), jnp.int32), pltpu.SemaphoreType.DMA((7,))],
        flops=42 * 128 * 128 * 512 * 2,
        vmem=24 * MIB,
    )
    keep, send = call(
        backward_far_kernel,
        [shape(4, 192, 512, dtype=F32), shape(4, 192, 512)],
        (*scalars, at, slots, *far, near, *sources),
        [SM] * 4 + [VM] * 4 + [ANY] * 8,
        [
            pltpu.VMEM((1024, 512), BF),
            pltpu.VMEM((1024, 512), F32),
            pltpu.VMEM((2, 1024, 512), BF),
            pltpu.VMEM((512, 512), F32),
            pltpu.SMEM((48,), jnp.int32),
            pltpu.SemaphoreType.DMA((8,)),
        ],
        flops=6 * 128 * 128 * 512 * 2 + 1024 * 512 * 512 * 4,
        vmem=24 * MIB,
    )
    came = hop(send, "core", C, 1)
    col_parts = call(
        core_sum_kernel,
        [shape(n, 512, dtype=F32 if k == 0 else BF) for n in (128, 64) for k in range(4)],
        (keep, came),
        [VM] * 2,
    )
    back, gw = col_parts[:4], col_parts[4:]
    gw_came = fan(gw, "x", X)

    sums = call(
        split_sum_kernel,
        [shape(128, 512, dtype=BF if d in (4, 5) else F32) for d in range(8)],
        (after(own, gw_came[0]), came_up, came_down),
        [VM] * 3,
    )
    from_left, from_right = ring_sum(sums)
    aggregated = (sums[0] + from_left.astype(F32) + from_right.astype(F32)).astype(BF)

    gw = total_of(gw[0], gw_came)
    gw = swap_sum(gw, "y", Y, (1, 2, 3), F32)
    grad_y = total_of(back[0], fan([after(v, gw) for v in back], "x", X))
    gw = swap_sum(gw, "z", Z, (1,), F32)
    grad_x = jnp.dot(grad_y, weight.T, precision=lax.Precision.HIGH, preferred_element_type=F32)
    gw = swap_sum(gw, "z", Z, (2, 4, 6), BF)
    gw = gw.astype(BF)
    gw = [gw, *fan([gw] * X, "x", X)]
    (grad_w,) = call(
        place_kernel,
        [shape(512, 512, dtype=F32)],
        (at, *gw, *[hop(v, "core", C, 1) for v in gw]),
        [SM] + [VM] * 8,
    )
    return aggregated, grad_x, grad_w


def solution(mesh):
    grid = Mesh(mesh.devices.reshape(X, C, Y, Z), ("x", "core", "y", "z"))
    col, row = ("x", "core"), ("y", "z")
    placed = (
        P(row + col, None),
        P(),
        P(col, row, None, None, None),
        P(col, row, None),
        P(col, row, None),
        P(col, row),
        P(col + row, None),
    )
    return jax.shard_map(
        shards,
        mesh=grid,
        in_specs=placed,
        out_specs=(P(col + row, None), P(row + col, None), P()),
        check_vma=False,
    )
```
